256 devices in a mesh: leaf: 16 (over z, core), row: 4 (over y), col: 4 (over x).
Axes of the slice: x: 4, y: 4, z: 8, core: 2. Of those that a mesh axis runs over, the one named last changes fastest.
Arguments:
- rhs: bfloat16 [79360, 512], P(('leaf', 'row'), 'col'), may hold values from -6 to 6
- pivot_inverse: bfloat16 [79360, 2560], P('leaf', 'row'), may hold values from -0.125 to 0.125
- panel: bfloat16 [46080, 2560], P('leaf', 'row'), may hold values from -0.0625 to 0.0625
- live: int32 [31], replicated, may hold values from 10 to 20, as said below
- parent_map: int32 [30, 12], replicated, may hold values from 0 to 19, as said below
Outputs:
- forward_solution: bfloat16 [79360, 512], P(('leaf', 'row'), 'col')
- solution: bfloat16 [79360, 512], P(('leaf', 'row'), 'col')
The draws below stay inside these ranges and needn't reach their ends.
Inputs may be any that keep to these rules, and one draw needn't show every extreme that they name: `live`: the root front (last index) is full, 20 blocks. `parent_map`: within one front's row the parent blocks are distinct.
All inputs are finite; a program needn't handle non-finite values.
Results may differ from the reference program's by a relative error of at most 0.012.
Values may be sent and summed in bfloat16 or wider, within the bound.
A program may use at most 64 MiB of HBM per device.

```python
import jax
import jax.numpy as jnp

F = 2560
E = 1536
R = 512
DEPTH = 4
FRONTS = 31
CHILDREN = 30
DPIECE = 4960
WPIECE = 2880
VPIECE = 1240
N_LEAF = 16
N_ROW = 4


def draw_live(key, part):
    counts = jax.random.randint(key, (FRONTS,), F // 256, F // 128 + 1)
    return counts.at[FRONTS - 1].set(F // 128).astype(jnp.int32)


def draw_parent_map(key, part):
    row_keys = jax.random.split(key, CHILDREN)

    def one_row(sub_key):
        return jax.random.permutation(sub_key, F // 128)[:E // 128]
    return jax.vmap(one_row)(row_keys).astype(jnp.int32)


def levels(stream_key, dims, shards, low, largest):
    def one(position, parts):
        heights = jax.random.uniform(jax.random.fold_in(jax.random.fold_in(stream_key, 6), position), (parts,), jnp.float32, low / len(shards), largest / len(shards))
        return jnp.repeat(jnp.exp(heights), dims[position] // parts).reshape((-1,) + (1,) * (len(dims) - position - 1))

    factor_of = one(*shards[0])
    for cut in shards[1:]:
        factor_of = factor_of * one(*cut)
    return factor_of


def bell_draw(rng, dims, spread, reach, cuts=(), kind=jnp.bfloat16):
    array = jax.random.normal(rng, dims, jnp.float32) * spread
    if len(cuts) > 0:
        array = levels(rng, dims, cuts, -0.22, 0.18) * array
    return jnp.clip(array, min=-reach, max=reach).astype(kind)


def setup_inputs(seed: int = 0) -> dict:
    arg_keys = jax.random.split(jax.random.key(seed), 6)
    return {
        "rhs": bell_draw(arg_keys[0], (N_LEAF * N_ROW * VPIECE, R), 1.0, 6.0, ((0, 64), (1, 4))),
        "pivot_inverse": bell_draw(arg_keys[1], (N_LEAF * DPIECE, F), F ** -0.5, 0.125, ((0, 16), (1, 4))),
        "panel": bell_draw(arg_keys[2], (N_LEAF * WPIECE, F), (4 * F) ** -0.5, 0.0625, ((0, 16), (1, 4))),
        "live": draw_live(jax.random.fold_in(arg_keys[5], 71), 0),
        "parent_map": draw_parent_map(jax.random.fold_in(arg_keys[5], 71), 0),
    }


def to_front(group_block):
    count_g, total_rows, row_width = group_block.shape
    piece_rows = total_rows // N_ROW
    return group_block.reshape(count_g, N_ROW, piece_rows, row_width).transpose(1, 0, 2, 3).reshape(count_g * total_rows, row_width)


def from_front(full_block, groups):
    total_rows, row_width = full_block.shape
    piece_rows = total_rows // (N_ROW * groups)
    return full_block.reshape(N_ROW, groups, piece_rows, row_width).transpose(1, 0, 2, 3)


def block_onehot(mapping):
    return (jnp.arange(F // 128, dtype=jnp.int32)[:, None] == mapping[None, :]).astype(jnp.float32)


def reference(rhs, pivot_inverse, panel, live, parent_map):
    vectors = rhs.reshape(N_LEAF, N_ROW, VPIECE, R)
    pivots = pivot_inverse.reshape(N_LEAF, DPIECE, F)
    panels = panel.reshape(N_LEAF, WPIECE, F)
    forward_out = jnp.zeros((N_LEAF, N_ROW, VPIECE, R), jnp.bfloat16)
    backward_out = jnp.zeros((N_LEAF, N_ROW, VPIECE, R), jnp.bfloat16)
    layout = []
    vec_off, piv_off, pan_off, front_base = 0, 0, 0, 0
    for level_no in range(DEPTH + 1):
        groups = 2 ** level_no
        layout.append((groups, vec_off, piv_off, pan_off, front_base))
        vec_off += F // (N_ROW * groups)
        piv_off += F // groups
        pan_off += E // groups
        front_base += N_LEAF // groups
    updates = {}
    forward_values = {}
    masks = {}
    for level_no in range(DEPTH + 1):
        groups, vec_off, piv_off, pan_off, front_base = layout[level_no]
        piece_rows = F // (N_ROW * groups)
        for front_no in range(N_LEAF // groups):
            lower_g = front_no * groups
            upper_g = lower_g + groups
            right_side = to_front(vectors[lower_g:upper_g, :, vec_off:vec_off + piece_rows].reshape(groups, N_ROW * piece_rows, R))
            if level_no > 0:
                child_base = layout[level_no - 1][4]
                incoming = jnp.zeros((F, R), jnp.float32)
                for side_no in range(2):
                    child_no = 2 * front_no + side_no
                    onehot = block_onehot(parent_map[child_base + child_no])
                    child_update = updates[(level_no - 1, child_no)].astype(jnp.float32).reshape(E // 128, 128, R)
                    incoming = incoming + jnp.einsum("ke,eab->kab", onehot, child_update).reshape(F, R)
                right_side = (right_side.astype(jnp.float32) - incoming).astype(jnp.bfloat16)
            live_mask = (jnp.arange(F, dtype=jnp.int32) < live[front_base + front_no] * 128)[:, None]
            masks[(level_no, front_no)] = live_mask
            masked = jnp.where(live_mask, right_side, jnp.zeros_like(right_side))
            diag_block = to_front(pivots[lower_g:upper_g, piv_off:piv_off + F // groups])
            product = jnp.dot(diag_block, masked, preferred_element_type=jnp.float32)
            forward_value = jnp.where(live_mask, product, 0.0).astype(jnp.bfloat16)
            forward_values[(level_no, front_no)] = forward_value
            if level_no < DEPTH:
                off_block = to_front(panels[lower_g:upper_g, pan_off:pan_off + E // groups])
                updates[(level_no, front_no)] = jnp.dot(off_block, masked, preferred_element_type=jnp.float32).astype(jnp.bfloat16)
            forward_out = forward_out.at[lower_g:upper_g, :, vec_off:vec_off + piece_rows].set(from_front(forward_value, groups))
    solved = {}
    for level_no in reversed(range(DEPTH + 1)):
        groups, vec_off, piv_off, pan_off, front_base = layout[level_no]
        piece_rows = F // (N_ROW * groups)
        for front_no in range(N_LEAF // groups):
            lower_g = front_no * groups
            upper_g = lower_g + groups
            diag_block = to_front(pivots[lower_g:upper_g, piv_off:piv_off + F // groups])
            value = jnp.dot(diag_block.T, forward_values[(level_no, front_no)], preferred_element_type=jnp.float32)
            if level_no < DEPTH:
                parent_value = solved[(level_no + 1, front_no // 2)].astype(jnp.float32).reshape(F // 128, 128, R)
                onehot = block_onehot(parent_map[front_base + front_no])
                taken_rows = jnp.einsum("ke,kab->eab", onehot, parent_value).reshape(E, R).astype(jnp.bfloat16)
                off_block = to_front(panels[lower_g:upper_g, pan_off:pan_off + E // groups])
                value = value - jnp.dot(off_block.T, taken_rows, preferred_element_type=jnp.float32)
            result = jnp.where(masks[(level_no, front_no)], value, 0.0).astype(jnp.bfloat16)
            solved[(level_no, front_no)] = result
            backward_out = backward_out.at[lower_g:upper_g, :, vec_off:vec_off + piece_rows].set(from_front(result, groups))
    return forward_out.reshape(N_LEAF * N_ROW * VPIECE, R), backward_out.reshape(N_LEAF * N_ROW * VPIECE, R)
```

```python
import jax
import jax.numpy as jnp
from jax import lax
from jax.experimental import pallas as pl
from jax.experimental.pallas import tpu as pltpu
from jax.sharding import PartitionSpec as P

MESH = pl.DeviceIdType.MESH
F32 = jnp.float32
BF16 = jnp.bfloat16

F = 2560
E = 1536
ROWS = 4
TOP = 4
Q = F // ROWS
H = Q // 2
EB = E // 128
C = 128

GROUPS = [2**k for k in range(TOP + 1)]
VOFF = [0, 640, 960, 1120, 1200]
DOFF = [0, 2560, 3840, 4480, 4800]
WOFF = [0, 1536, 2304, 2688]
BASE = [0, 16, 24, 28, 30]


def pad16(n):
    return (n + 15) // 16 * 16


def scratch_shapes():
    shapes = {}
    for k in range(TOP + 1):
        g = GROUPS[k]
        shapes[f"d{k}"] = ((F // g, Q), BF16)
        shapes[f"x{k}"] = ((Q, C), BF16)
        shapes[f"dty{k}"] = ((Q, C), F32)
        shapes[f"v{k}"] = ((F // g, C), BF16)
        shapes[f"vr{k}"] = ((3, Q // g if k < TOP else F // g, C), BF16)
        shapes[f"y{k}"] = ((F // g, C), BF16)
        if 0 < k < TOP:
            shapes[f"b{k}"] = ((Q, C), BF16)
        if k < TOP:
            shapes[f"w{k}"] = ((E // g, Q), BF16)
            shapes[f"u{k}"] = ((E // g, C), BF16)
            shapes[f"p{k}"] = ((F, C), BF16)
            shapes[f"pr{k}"] = ((ROWS, H, C), BF16)
            shapes[f"ys{k}"] = ((ROWS, H, C), BF16)
            shapes[f"yr{k}"] = ((3, H, C), BF16)
            shapes[f"c{k}"] = ((2, H, C), BF16)
            shapes[f"t{k}"] = ((E // g, C), BF16)
        if k > 0:
            shapes[f"bp{k}"] = ((2, H, C), BF16)
            shapes[f"bpr{k}"] = ((H, C), BF16)
            shapes[f"s{k}"] = ((F, C), BF16)
    for name, n in (("f1", 2), ("f2", 4), ("f3", 8), ("r4", 8), ("r3", 4), ("r2", 2)):
        if n == 2:
            shapes[f"zs_{name}"] = ((H, C), BF16)
            shapes[f"zr_{name}"] = ((H, C), BF16)
        else:
            pch = pad16(H // n)
            shapes[f"zs_{name}"] = ((n, pch, C), BF16)
            shapes[f"zr_{name}"] = ((n - 1, pch, C), BF16)
            shapes[f"zg_{name}"] = ((n, pch, C), BF16)
    shapes["b4s"] = ((16, 48, C), BF16)
    shapes["b4"] = ((Q, C), F32)
    shapes["half"] = ((H, C), F32)
    shapes["acc"] = ((Q, C), F32)
    shapes["fin"] = ((F // 16, C), F32)
    return shapes


SHAPES = scratch_shapes()
NAMES = list(SHAPES)
N_REMOTE = 200
N_LOCAL = 9


def kernel(rhs, piv, pan, live, pmap, fwd, sol, *refs):
    S = dict(zip(NAMES, refs))
    send_sem, recv_sem, load_sem = refs[len(NAMES) :]
    leaf = lax.axis_index("leaf")
    row = lax.axis_index("row")
    par = leaf % 2
    chip = leaf // 2
    counter = [0]
    unsent = []

    def xor(a, m):
        return a + m - 2 * (a & m)

    def send(src, dst, device):
        i = counter[0]
        counter[0] += 1
        copy = pltpu.make_async_remote_copy(
            src_ref=src,
            dst_ref=dst,
            send_sem=send_sem.at[i],
            recv_sem=recv_sem.at[i],
            device_id=device,
            device_id_type=MESH,
        )
        copy.start()
        unsent.append(copy)
        return copy

    def to_leaf(src, dst, m):
        return send(src, dst, {"leaf": xor(leaf, m)})

    def to_row(src, dst, m):
        return send(src, dst, {"row": xor(row, m)})

    loads = {}
    order = [("w0", pan, 0), ("d0", piv, 0), ("w1", pan, 1), ("d1", piv, 1), ("w2", pan, 2), ("d2", piv, 2)]
    order += [("w3", pan, 3), ("d3", piv, 3), ("d4", piv, 4)]
    for n, (name, ref, k) in enumerate(order):
        rows = S[name].shape[0]
        off = (WOFF if ref is pan else DOFF)[k]
        copy = pltpu.make_async_copy(ref.at[pl.ds(off, rows)], S[name], load_sem.at[n])
        copy.start()
        loads[name] = copy

    barrier = pltpu.get_barrier_semaphore()
    for m in range(1, 16):
        pl.semaphore_signal(barrier, inc=1, device_id={"leaf": xor(leaf, m)}, device_id_type=MESH)
    for m in range(1, ROWS):
        pl.semaphore_signal(barrier, inc=1, device_id={"row": xor(row, m)}, device_id_type=MESH)

    def live_rows(k):
        return live[BASE[k] + leaf // GROUPS[k]] * 128

    def below(n, start, k):
        return (lax.broadcasted_iota(jnp.int32, (n, C), 0) + start) < live_rows(k)

    def targets(k):
        g = GROUPS[k]
        t = leaf % g
        child = BASE[k] + leaf // g
        found = {}
        for r in range(ROWS):
            for j in range(3):
                block = pmap[child, 3 * r + (3 * t + j) // g]
                found[r, j] = jnp.full((16, C), block.astype(F32), F32).astype(BF16)
        return found

    def place(k):
        g = GROUPS[k]
        n = 128 // g
        u, p = S[f"u{k}"], S[f"p{k}"]
        found = targets(k)
        groups = [range(3)] if g == 1 else [[0], [1], [2]]

        def body(i, carry):
            for js in groups:
                at = ((3 * (leaf % g) + js[0]) % g) * n + i * 16
                vals = {
                    (r, j): u[pl.ds(pl.multiple_of((3 * r + j) * n + i * 16, 16), 16), :]
                    for r in range(ROWS)
                    for j in js
                }
                for b in range(F // 128):
                    where = pl.ds(pl.multiple_of(b * 128 + at, 16), 16)
                    out = p[where, :] if g == 2 else jnp.zeros((16, C), BF16)
                    for key, val in vals.items():
                        out = jnp.where(found[key] == BF16(b), val, out)
                    p[where, :] = out
            return carry

        lax.fori_loop(0, n // 16, body, 0)

    def pick(k):
        g = GROUPS[k]
        n = 128 // g
        s, w = S[f"s{k + 1}"], S[f"t{k}"]
        found = targets(k)

        def body(i, carry):
            for js in [range(3)] if g == 1 else [[0], [1], [2]]:
                at = ((3 * (leaf % g) + js[0]) % g) * n + i * 16
                keys = [(r, j) for r in range(ROWS) for j in js]
                outs = {key: jnp.zeros((16, C), BF16) for key in keys}
                for b in range(F // 128):
                    val = s[pl.ds(pl.multiple_of(b * 128 + at, 16), 16), :]
                    for key in keys:
                        outs[key] = jnp.where(found[key] == BF16(b), val, outs[key])
                for r, j in keys:
                    w[pl.ds(pl.multiple_of((3 * r + j) * n + i * 16, 16), 16), :] = outs[r, j]
            return carry

        lax.fori_loop(0, n // 16, body, 0)

    def product(dst, mat, x, chunk):
        rows = mat.shape[0]
        chunk = min(chunk, rows)
        val = x[...]
        if chunk == rows:
            dst[pl.ds(0, rows), :] = jnp.dot(mat[...], val, preferred_element_type=F32).astype(BF16)
            return

        def body(i, carry):
            at = pl.multiple_of(i * chunk, chunk)
            dst[pl.ds(at, chunk), :] = jnp.dot(
                mat[pl.ds(at, chunk), :], val, preferred_element_type=F32
            ).astype(BF16)
            return carry

        lax.fori_loop(0, rows // chunk, body, 0)

    def transposed(dst, mat, x, less=None):
        def body(i, carry):
            at = pl.multiple_of(i * 128, 128)
            out = lax.dot_general(
                mat[:, pl.ds(at, 128)], x[...], (((0,), (0,)), ((), ())), preferred_element_type=F32
            )
            if less is not None:
                out = less[pl.ds(at, 128), :] - out
            dst[pl.ds(at, 128), :] = out
            return carry

        lax.fori_loop(0, Q // 128, body, 0)

    def chip_sum(name, n, half):
        if n == 1:
            return
        zs, zr = S[f"zs_{name}"], S[f"zr_{name}"]
        if n == 2:
            zs[...] = half[...].astype(BF16)
            copy = to_leaf(zs, zr, 2)
            copy.wait_recv()
            half[...] = zs[...].astype(F32) + zr[...].astype(F32)
            return
        zg = S[f"zg_{name}"]
        ch = H // n
        mine = chip % n
        for j in range(n):
            zs[j, 0:ch, :] = half[j * ch : (j + 1) * ch, :].astype(BF16)
        copies = [to_leaf(zs.at[xor(mine, m)], zr.at[m - 1], 2 * m) for m in range(1, n)]
        total = zs[mine].astype(F32)
        for m in range(1, n):
            copies[m - 1].wait_recv()
            total = total + zr[m - 1].astype(F32)
        zg[mine] = total.astype(BF16)
        copies = [to_leaf(zg.at[mine], zg.at[mine], 2 * m) for m in range(1, n)]
        for copy in copies:
            copy.wait_recv()
        for j in range(n):
            half[j * ch : (j + 1) * ch, :] = zg[j, 0:ch, :].astype(F32)

    v_copies = {}
    y_copies = {}

    def send_v(k):
        h = Q // GROUPS[k]
        v_copies[k] = [
            to_row(S[f"v{k}"].at[pl.ds(pl.multiple_of(xor(row, m) * h, h), h)], S[f"vr{k}"].at[m - 1], m)
            for m in range(1, ROWS)
        ]

    def finish_v(k):
        g = GROUPS[k]
        h = Q // g
        at = pl.multiple_of(row * h, h)
        total = S[f"v{k}"][pl.ds(at, h), :].astype(F32)
        for m in range(1, ROWS):
            v_copies[k][m - 1].wait_recv()
            total = total + S[f"vr{k}"][m - 1].astype(F32)
        piece = jnp.where(below(h, (row * g + leaf % g) * h, k), total, 0.0).astype(BF16)
        fwd[VOFF[k] : VOFF[k] + h, :] = piece
        y = S[f"y{k}"]
        y[pl.ds(at, h), :] = piece
        y_copies[k] = [to_row(y.at[pl.ds(at, h)], y.at[pl.ds(at, h)], m) for m in range(1, ROWS)]

    def finish_y(k):
        for copy in y_copies[k]:
            copy.wait_recv()
        transposed(S[f"dty{k}"], S[f"d{k}"], S[f"y{k}"])

    for k in range(1, TOP):
        S[f"p{k}"][...] = jnp.zeros((F, C), BF16)
    S["x0"][...] = jnp.where(below(Q, row * Q, 0), rhs[0:Q, :], jnp.zeros((Q, C), BF16))

    b_copies = {}
    for k in range(1, TOP):
        h = Q // GROUPS[k]
        S[f"b{k}"][pl.ds(pl.multiple_of((leaf % GROUPS[k]) * h, h), h), :] = rhs[VOFF[k] : VOFF[k] + h, :]
    S["b4s"][leaf, 0:40, :] = rhs[1200:1240, :]
    S["b4s"][leaf, 32:48, :] = jnp.concatenate([rhs[1232:1240, :], jnp.zeros((8, C), BF16)], 0)

    pl.semaphore_wait(barrier, 18)

    for k in range(1, TOP):
        g = GROUPS[k]
        h = Q // g
        mine = pl.ds(pl.multiple_of((leaf % g) * h, h), h)
        b_copies[k] = [to_leaf(S[f"b{k}"].at[mine], S[f"b{k}"].at[mine], m) for m in range(1, g)]
    b_copies[4] = [to_leaf(S["b4s"].at[leaf], S["b4s"].at[leaf], m) for m in range(1, 16)]

    for k in range(TOP):
        g = GROUPS[k]
        u, p, pr, ys, yr, c = (S[f"{name}{k}"] for name in ("u", "p", "pr", "ys", "yr", "c"))
        loads[f"w{k}"].wait()
        product(u, S[f"w{k}"], S[f"x{k}"], 384)
        place(k)
        pairs = [
            to_leaf(p.at[pl.ds(pl.multiple_of(r * Q + (1 - par) * H, 16), H)], pr.at[r], 1) for r in range(ROWS)
        ]
        loads[f"d{k}"].wait()
        product(S[f"v{k}"], S[f"d{k}"], S[f"x{k}"], 640)
        for r in range(ROWS):
            pairs[r].wait_recv()
            own = p[pl.ds(pl.multiple_of(r * Q + par * H, 16), H), :]
            ys[r] = (own.astype(F32) + pr[r].astype(F32)).astype(BF16)
        copies = [to_row(ys.at[xor(row, m)], yr.at[m - 1], m) for m in range(1, ROWS)]
        send_v(k)
        if k >= 1:
            finish_v(k - 1)
        if k >= 2:
            finish_y(k - 2)
        for copy in b_copies[k + 1]:
            copy.wait_recv()
        if k + 1 == TOP:
            for j in range(16):
                S["b4"][40 * j : 40 * j + 40, :] = S["b4s"][j, 0:40, :].astype(F32)
        total = ys[row].astype(F32)
        for m in range(1, ROWS):
            copies[m - 1].wait_recv()
            total = total + yr[m - 1].astype(F32)
        half = S["half"]
        half[...] = total
        chip_sum(f"f{k}", g, half)
        c[par] = half[...].astype(BF16)
        pair = to_leaf(c.at[par], c.at[par], 1)
        pair.wait_recv()
        b = S[f"b{k + 1}"]
        for s in range(2):
            x = b[s * H : (s + 1) * H, :].astype(F32) - c[s].astype(F32)
            x = jnp.where(below(H, row * Q + s * H, k + 1), x, 0.0)
            S[f"x{k + 1}"][s * H : (s + 1) * H, :] = x.astype(BF16)

    loads["d4"].wait()
    n = F // 16
    v = S["v4"]
    product(v, S["d4"], S["x4"], n)
    copies = [to_row(v, S["vr4"].at[m - 1], m) for m in range(1, ROWS)]
    finish_v(3)
    finish_y(2)
    total = v[...].astype(F32)
    for m in range(1, ROWS):
        copies[m - 1].wait_recv()
        total = total + S["vr4"][m - 1].astype(F32)
    S["fin"][...] = total
    for r in range(ROWS):
        at = (r * 16 + leaf) * 40
        S["fin"][r * 40 : r * 40 + 40, :] = jnp.where(below(40, at, 4), S["fin"][r * 40 : r * 40 + 40, :], 0.0)
    S["y4"][...] = S["fin"][...].astype(BF16)
    fwd[1200:1240, :] = S["fin"][pl.ds(pl.multiple_of(row * 40, 8), 40), :].astype(BF16)
    acc = S["acc"]
    transposed(acc, S["d4"], S["y4"])

    for k in range(TOP, 0, -1):
        g = GROUPS[k]
        h = Q // g
        if k < TOP:
            pick(k)
            transposed(acc, S[f"w{k}"], S[f"t{k}"], S[f"dty{k}"])
        bp, bpr, s = S[f"bp{k}"], S[f"bpr{k}"], S[f"s{k}"]
        for i in range(2):
            bp[i] = acc[i * H : (i + 1) * H, :].astype(BF16)
        pair = to_leaf(bp.at[1 - par], bpr, 1)
        if k == TOP:
            finish_y(3)
        pair.wait_recv()
        half = S["half"]
        half[...] = acc[pl.ds(pl.multiple_of(par * H, H), H), :] + bpr[...].astype(F32)
        chip_sum(f"r{k}", g // 2, half)
        def part(r, i):
            return s.at[pl.ds(pl.multiple_of(r * Q + i * H, 16), H)]

        own = part(row, par)
        own[...] = jnp.where(below(H, row * Q + par * H, k), half[...], 0.0).astype(BF16)
        copies = [to_row(own, own, m) for m in range(1, ROWS)]
        pairs = [to_leaf(own, own, 1)]
        for m in range(1, ROWS):
            copies[m - 1].wait_recv()
            block = part(xor(row, m), par)
            pairs.append(to_leaf(block, block, 1))
        for copy in pairs:
            copy.wait_recv()
        if k == TOP:
            acc[...] = s[pl.ds(pl.multiple_of(row * Q, 16), Q), :].astype(F32)
            sol[1200:1240, :] = acc[pl.ds(pl.multiple_of(leaf * 40, 8), 40), :].astype(BF16)
        else:
            sol[VOFF[k] : VOFF[k] + h, :] = s[pl.ds(pl.multiple_of(row * Q + (leaf % g) * h, 16), h), :]
    pick(0)
    transposed(acc, S["w0"], S["t0"], S["dty0"])
    sol[0:Q, :] = jnp.where(below(Q, row * Q, 0), acc[...], 0.0).astype(BF16)

    for copy in unsent:
        copy.wait_send()


def on_device(rhs, pivot_inverse, panel, live, parent_map):
    shape = jax.ShapeDtypeStruct(rhs.shape, BF16)
    vmem = pl.BlockSpec(memory_space=pltpu.VMEM)
    smem = pl.BlockSpec(memory_space=pltpu.SMEM)
    hbm = pl.BlockSpec(memory_space=pl.ANY)
    return pl.pallas_call(
        kernel,
        out_shape=(shape, shape),
        in_specs=[vmem, hbm, hbm, smem, smem],
        out_specs=(vmem, vmem),
        scratch_shapes=[pltpu.VMEM(*SHAPES[name]) for name in NAMES]
        + [
            pltpu.SemaphoreType.DMA((N_REMOTE,)),
            pltpu.SemaphoreType.DMA((N_REMOTE,)),
            pltpu.SemaphoreType.DMA((N_LOCAL,)),
        ],
        compiler_params=pltpu.CompilerParams(collective_id=0, has_side_effects=True),
    )(rhs, pivot_inverse, panel, live, parent_map)


def solution(mesh):
    in_specs = (P(("leaf", "row"), "col"), P("leaf", "row"), P("leaf", "row"), P(), P())
    out_specs = (P(("leaf", "row"), "col"), P(("leaf", "row"), "col"))
    return jax.shard_map(
        on_device, mesh=mesh, in_specs=in_specs, out_specs=out_specs, check_vma=False
    )
```
